512 devices in a mesh: lon: 64 (over x, y_hi, z), lat: 8 (over y_lo, core).
Axes of the slice: x: 4, y: 8 (y_hi: 2, y_lo: 4; y = y_hi * 4 + y_lo), z: 8, core: 2. Of those that a mesh axis runs over, the one named last changes fastest.
Arguments:
- fields: bfloat16 [2048, 512, 256], P('lon', 'lat'), may hold values from -48 to 48
Outputs:
- coarse_fluxes: bfloat16 [2048, 512, 256], P('lon', 'lat')
- snapshot_gram: float32 [64, 64], replicated
The draws below stay inside these ranges and needn't reach their ends.
All inputs are finite; a program needn't handle non-finite values.
Results may differ from the reference program's by a relative error of at most 0.0064.
Values may be sent and summed in bfloat16 or wider, within the bound.
A program may use at most 64 MiB of HBM per device.

```python
import math
import jax
import jax.numpy as jnp
from jax import lax

SNAP = 64
R = 128
CLON = 32
CLAT = 64
NLON = 2048
NLAT = 512
N_LON = 64
N_LAT = 8


def draw_fields(key, part):
    keys = jax.random.split(key, 6)
    phases = jax.random.uniform(keys[0], (3, SNAP), jnp.float32, 0.0, 2.0 * math.pi)
    signs = jax.random.rademacher(keys[2], (4, SNAP)).astype(jnp.float32)
    coefs = jax.random.uniform(keys[1], (4, SNAP), jnp.float32, 0.02, 0.06) * signs
    lon_angle = jnp.arange(NLON, dtype=jnp.float32)[:, None, None] / NLON * (2.0 * math.pi)
    lat_frac = jnp.arange(NLAT, dtype=jnp.float32)[None, :, None] / NLAT
    log_envelope = 0.3 * jnp.sin(lon_angle + phases[0]) + 0.2 * jnp.sin(3.0 * lon_angle + phases[1])
    log_envelope = log_envelope + 0.3 * lat_frac + 0.2 * jnp.sin(4.0 * math.pi * lat_frac + phases[2])
    common = jax.random.normal(keys[3], (NLON, NLAT, SNAP), jnp.float32)
    noise = jax.random.normal(keys[4], (NLON, NLAT, 4 * SNAP), jnp.float32)
    cell_scale = jnp.exp(jax.random.uniform(keys[5], (NLON, NLAT, 1), jnp.float32, -0.4, 0.4))
    amplitude = 0.9 * math.sqrt(R)
    envelope = amplitude * jnp.exp(log_envelope) * cell_scale
    values = jnp.tile(envelope, (1, 1, 4)) * (coefs.reshape(4 * SNAP) * jnp.tile(common, (1, 1, 4)) + noise)
    return jnp.clip(values, -48.0, 48.0).astype(jnp.bfloat16)


def setup_inputs(seed: int = 0) -> dict:
    key_list = jax.random.split(jax.random.key(seed), 2)
    return {
        "fields": draw_fields(jax.random.fold_in(key_list[1], 71), 0),
    }


def tap_values(distance):
    weight = jnp.exp(-(distance.astype(jnp.float32) / R) ** 2)
    return jnp.where(jnp.abs(distance) <= R, weight, 0.0).astype(jnp.bfloat16)


def flux_products(values):
    left_side = jnp.concatenate([values[:, :, :3 * SNAP], values[:, :, :SNAP]], axis=2)
    right_side = jnp.concatenate([values[:, :, 3 * SNAP:]] * 3 + [values[:, :, SNAP:2 * SNAP]], axis=2)
    return (left_side.astype(jnp.float32) * right_side.astype(jnp.float32)).astype(jnp.bfloat16)


def reference(fields):
    offsets = jnp.arange(-R, R + 1).astype(jnp.int32)
    lon_norm = jnp.sum(tap_values(offsets).astype(jnp.float32))
    band_ids = (jnp.arange(3 * R)[None, :] - R - jnp.arange(R)[:, None]).astype(jnp.int32)
    near_taps = tap_values(band_ids).astype(jnp.float32).reshape(R, 3, R).transpose(1, 0, 2)
    block_count = NLON // R

    def lon_pass(rows_in):
        products = flux_products(rows_in)
        blocks = products.reshape(block_count, R, CLAT * 4 * SNAP).astype(jnp.float32)
        summed = jnp.einsum("ij,bjk->bik", near_taps[0], jnp.roll(blocks, 1, 0), precision=lax.Precision.HIGHEST)
        summed = summed + jnp.einsum("ij,bjk->bik", near_taps[1], blocks, precision=lax.Precision.HIGHEST)
        summed = summed + jnp.einsum("ij,bjk->bik", near_taps[2], jnp.roll(blocks, -1, 0), precision=lax.Precision.HIGHEST)
        return (summed / lon_norm).astype(jnp.bfloat16).reshape(NLON, CLAT, 4 * SNAP)

    lat_major = fields.reshape(NLON, N_LAT, CLAT, 4 * SNAP).transpose(1, 0, 2, 3)
    smoothed = lax.map(lon_pass, lat_major)
    smoothed = smoothed.transpose(1, 0, 2, 3).reshape(NLON, NLAT, 4 * SNAP)
    lat_distance = (jnp.arange(NLAT)[None, :] - jnp.arange(NLAT)[:, None]).astype(jnp.int32)
    lat_taps = tap_values(lat_distance).astype(jnp.float32)
    lat_norm = jnp.sum(lat_taps, axis=1)

    def lat_pass(columns):
        summed = jnp.einsum("yz,xzc->xyc", lat_taps, columns.astype(jnp.float32), precision=lax.Precision.HIGHEST)
        coarse_part = (summed / lat_norm[None, :, None]).astype(jnp.bfloat16)
        rows_flat = coarse_part.astype(jnp.float32).reshape(-1, SNAP)
        return coarse_part, jnp.dot(rows_flat.T, rows_flat, precision=lax.Precision.HIGHEST)

    coarse_parts, gram_parts = lax.map(lat_pass, smoothed.reshape(N_LON, CLON, NLAT, 4 * SNAP))
    coarse_fluxes = coarse_parts.reshape(NLON, NLAT, 4 * SNAP)
    snapshot_gram = jnp.sum(gram_parts, axis=0) / (4 * NLON * NLAT)
    return coarse_fluxes, snapshot_gram
```

```python
import numpy as np
import jax
import jax.numpy as jnp
from jax import lax
from jax.experimental import pallas as pl
from jax.experimental.pallas import tpu as pltpu
from jax.sharding import Mesh
from jax.sharding import PartitionSpec as P

AXES = ("X", "H", "Z", "L", "C")
LON = ("X", "H", "Z")
LAT = ("L", "C")
R = 128
NX, NY, NZ = 4, 8, 8
ROWS, LANES = 16, 128
MESH_ID = pl.DeviceIdType.MESH
F32, BF16 = jnp.float32, jnp.bfloat16
NT = (((1,), (1,)), ((), ()))


def taps(distance):
    weight = jnp.exp(-((distance.astype(F32) / R) ** 2))
    return jnp.where(jnp.abs(distance) <= R, weight, 0.0)


def lon_norm():
    d = np.arange(-R, R + 1).astype(np.float32)
    return float(np.sum(np.exp(-((d / R) ** 2)).astype(BF16).astype(np.float32)))


def iota(shape, axis):
    return lax.broadcasted_iota(jnp.int32, shape, axis)


def identity(n):
    return jnp.where(iota((n, n), 0) == iota((n, n), 1), 1.0, 0.0).astype(BF16)


def kernel(
    fields, out, gram,
    T, SA, SB, R1A, R1B, R2A, R2B, HA, HB, XO, XH, SM, AO, AH, W, OA, OB, Q1A, Q1B, FA, FB, MB, GA,
    g_part, g_core, g_z, g_y, g_x, g_end,
    loc, a1s, b1s, a1r, b1r, a2s, b2s, a2r, b2r, hs, hr, a3s, b3s, a3r, b3r, a4s, b4s, a4r, b4r, gs, gr,
):
    x, h, z = lax.axis_index("X"), lax.axis_index("H"), lax.axis_index("Z")
    l, c = lax.axis_index("L"), lax.axis_index("C")
    y = h * 4 + l
    yc = y * 2 + c

    def at_z(d):
        return {"Z": (z + d) % NZ}

    def at_yc(dy, dc):
        yy = (y + dy) % NY
        return {"H": yy // 4, "L": yy % 4, "C": (c + dc) % 2}

    def send(src, dst, ssem, rsem, device):
        pltpu.make_async_remote_copy(src, dst, ssem, rsem, device_id=device, device_id_type=MESH_ID).start()

    def wait(ref, sem):
        pltpu.make_async_copy(ref, ref, sem).wait()

    def local(src, dst, k):
        copy = pltpu.make_async_copy(src, dst, loc.at[k])
        copy.start()
        return copy

    z_offsets = [1, 7, 6, 5, 4, 3, 2]
    yc_offsets = [(dy, dc) for dy in (1, 7, 6, 5, 4, 3, 2, 0) for dc in (0, 1) if (dy, dc) != (0, 0)]

    barrier = pltpu.get_barrier_semaphore()
    for d in z_offsets:
        pl.semaphore_signal(barrier, inc=1, device_id=at_z(d), device_id_type=MESH_ID)
    for dy, dc in yc_offsets:
        pl.semaphore_signal(barrier, inc=1, device_id=at_yc(dy, dc), device_id_type=MESH_ID)
    for d in (1, 2, 3):
        pl.semaphore_signal(barrier, inc=1, device_id={"X": (x + d) % NX}, device_id_type=MESH_ID)

    eye = identity(256)

    def to_channels(t, carry):
        cells = fields[pl.ds(t * 2, 2)].reshape(128, 256)
        f = lax.dot_general(eye, cells, NT, preferred_element_type=F32)
        u, v, w, b = f[0:64], f[64:128], f[128:192], f[192:256]
        base = pl.multiple_of(t * 256, 256)
        T[pl.ds(base, 64), :] = u * b
        T[pl.ds(base + 64, 64), :] = v * b
        T[pl.ds(base + 128, 64), :] = w * b
        T[pl.ds(base + 192, 64), :] = u * v
        return carry

    lax.fori_loop(0, 16, to_channels, 0)

    def pack(k, carry):
        for j in range(8):
            ch = k * 8 + j
            SA[ch] = T[pl.ds(ch, 16, stride=256), :].astype(BF16)
            SB[ch] = T[pl.ds(ch + 128, 16, stride=256), :].astype(BF16)
        return carry

    lax.fori_loop(0, 16, pack, 0)
    pl.semaphore_wait(barrier, 25)

    for d in z_offsets:
        i = (1 - d) % 8
        send(SA.at[pl.ds(((z + d) % NZ) * 16, 16)], R1A.at[i], a1s, a1r.at[i // 4], at_z(d))
    own_a1 = local(SA.at[pl.ds(z * 16, 16)], R1A.at[1], 0)
    for dy, dc in yc_offsets:
        i = (1 - dy) % 8
        to = ((y + dy) % NY) * 2 + (c + dc) % 2
        send(SB.at[pl.ds(to * 8, 8)], R1B.at[2 * i + c], b1s, b1r.at[i // 4], at_yc(dy, dc))
    own_b1 = local(SB.at[pl.ds(yc * 8, 8)], R1B.at[2 + c], 1)

    def lon_matrix(k, carry):
        for block, shift in ((0, 0), (1, -1), (2, 1)):
            row = iota((32, 256), 0) + k * 32
            AO[pl.ds(block * 256 + k * 32, 32), :] = taps(2 * (iota((32, 256), 1) - row) + shift).astype(BF16)
            col = iota((32, 128), 1)
            col = jnp.where(col < 64, col - 64, col + 192)
            row = iota((32, 128), 0) + k * 32
            AH[pl.ds(block * 256 + k * 32, 32), :] = taps(2 * (col - row) + shift).astype(BF16)
        return carry

    lax.fori_loop(0, 8, lon_matrix, 0)

    def lat_matrix(k, carry):
        src = iota((32, 256), 0) + k * 32
        dst = iota((32, 256), 1)
        same = (src // 64) % 2 == (dst // 64) % 2
        apart = 64 * (src // 128 - dst // 128) + src % 64 - dst % 64
        for step in range(3):
            W[step, pl.ds(k * 32, 32), :] = jnp.where(same, taps(apart - 128 * (step - 1)), 0.0).astype(BF16)
        return carry

    lax.fori_loop(0, 8, lat_matrix, 0)
    ones = jnp.ones((16, 256), BF16)
    lat_sums = [jnp.dot(ones, W[k], preferred_element_type=F32)[0:1] for k in range(3)]
    inv_lat = []
    for dst in range(4):
        total = lat_sums[1]
        if dst > 0:
            total = total + lat_sums[2]
        if dst < 3:
            total = total + lat_sums[0]
        inv_lat.append(1.0 / total)
    inv_lon = 1.0 / lon_norm()

    own2 = []
    for g in (0, 1):
        if g == 0:
            own_a1.wait()
            wait(R1A.at[pl.ds(0, 3)], a1r.at[0])
        else:
            wait(R1A.at[pl.ds(0, 4)], a1r.at[1])
        for dy, dc in yc_offsets:
            to = ((y + dy) % NY) * 2 + (c + dc) % 2
            send(R1A.at[pl.ds(4 * g, 4), to], R2A.at[yc, pl.ds(4 * g, 4)], a2s, a2r.at[g], at_yc(dy, dc))
        own2.append(local(R1A.at[pl.ds(4 * g, 4), yc], R2A.at[yc, pl.ds(4 * g, 4)], 2 + g))
        if g == 0:
            own_b1.wait()
            wait(R1B.at[pl.ds(0, 7)], b1r.at[0])
        else:
            wait(R1B.at[pl.ds(0, 8)], b1r.at[1])
        for d in z_offsets:
            send(R1B.at[pl.ds(8 * g, 8), (z + d) % NZ], R2B.at[z, pl.ds(8 * g, 8)], b2s, b2r.at[g], at_z(d))
        own2.append(local(R1B.at[pl.ds(8 * g, 8), z], R2B.at[z, pl.ds(8 * g, 8)], 4 + g))

    for g in (0, 1):
        own2[2 * g].wait()
        wait(R2A.at[pl.ds(0, 15), pl.ds(0, 4)], a2r.at[g])
        for i in range(4 * g, 4 * g + 4):
            zz = (z + i + 7) % NZ
            hi = zz // 4
            send(R2A.at[pl.ds(hi * 8, 8), i], HA.at[hi, zz % 4], hs.at[0], hr.at[0], {"X": (x + 2 * hi + 3) % NX})
        own2[2 * g + 1].wait()
        wait(R2B.at[pl.ds(0, 7), pl.ds(0, 8)], b2r.at[g])
        for i in range(4 * g, 4 * g + 4):
            yy = (y + i + 7) % NY
            hi = yy // 4
            send(
                R2B.at[pl.ds(hi * 4, 4), pl.ds(2 * i, 2)],
                HB.at[hi, :, pl.ds((yy % 4) * 2, 2)],
                hs.at[1], hr.at[1], {"X": (x + 2 * hi + 3) % NX},
            )

    def filtered(tile_of, halo, halo_sem, store):
        def gather(lam, carry):
            for mu in range(8):
                XO[pl.ds(pl.multiple_of(lam * 16, 16), 16), mu * 128 : mu * 128 + 128] = tile_of(lam, mu)
            return carry

        lax.fori_loop(0, 16, gather, 0)
        wait(halo, halo_sem)
        for hi in (0, 1):
            for zz in range(4):
                for mu in range(8):
                    row = (1 - hi) * 64 + zz * 16
                    XH[row : row + 16, mu * 128 : mu * 128 + 128] = halo[hi, zz, mu]
        first = iota((256, 128), 1) < 64
        for n in range(8):
            cols = slice(n * 128, n * 128 + 128)
            if n % 2 == 0:
                wide = slice(n * 128, n * 128 + 256)
                zs = jnp.dot(AO[...], XO[:, wide], preferred_element_type=F32)
                zs = zs + jnp.dot(AH[...], XH[:, wide], preferred_element_type=F32)
            part = zs[:, (n % 2) * 128 : (n % 2) * 128 + 128]
            other = jnp.where(first, part[256:512], part[512:768])
            total = part[0:256] + pltpu.roll(other, 64, 1)
            SM[:, cols] = (total * inv_lon).astype(BF16)
        for dst in range(4):
            total = None
            for src in range(max(0, dst - 1), min(3, dst + 1) + 1):
                term = jnp.dot(SM[:, src * 256 : src * 256 + 256], W[dst - src + 1], preferred_element_type=F32)
                total = term if total is None else total + term
            total = (total * inv_lat[dst]).astype(BF16)
            for lam in range(16):
                for half in range(2):
                    store(lam, 2 * dst + half, total[lam * 16 : lam * 16 + 16, half * 128 : half * 128 + 128])

    def store_a(lam, mu, tile):
        OA[(lam // 8) * 8 + mu, (lam % 8 - z + 9) % NZ] = tile

    def store_b(lam, mu, tile):
        OB[lam % 8, 2 * (((lam // 8) * 4 + mu // 2 - y + 9) % NY) + mu % 2] = tile

    filtered(lambda lam, mu: R2A[(lam // 8) * 8 + mu, (lam % 8 - z + 9) % NZ], HA, hr.at[0], store_a)
    own3 = {}
    for g in (1, 0):
        for dy, dc in yc_offsets:
            to = ((y + dy) % NY) * 2 + (c + dc) % 2
            send(OA.at[to, pl.ds(4 * g, 4)], Q1A.at[yc, pl.ds(4 * g, 4)], a3s, a3r.at[g], at_yc(dy, dc))
        own3["a", g] = local(OA.at[yc, pl.ds(4 * g, 4)], Q1A.at[yc, pl.ds(4 * g, 4)], 6 + g)
    filtered(
        lambda lam, mu: R2B[lam % 8, 2 * (((lam // 8) * 4 + mu // 2 - y + 9) % NY) + mu % 2], HB, hr.at[1], store_b
    )
    for g in (1, 0):
        for d in z_offsets:
            send(OB.at[(z + d) % NZ, pl.ds(8 * g, 8)], Q1B.at[z, pl.ds(8 * g, 8)], b3s, b3r.at[g], at_z(d))
        own3["b", g] = local(OB.at[z, pl.ds(8 * g, 8)], Q1B.at[z, pl.ds(8 * g, 8)], 8 + g)

    own4 = []
    for g in (1, 0):
        own3["a", g].wait()
        wait(Q1A.at[pl.ds(0, 15), pl.ds(0, 4)], a3r.at[g])
        for k in range(4 * g, 4 * g + 4):
            d = (k - 1) % 8
            if d:
                send(Q1A.at[:, k], FA.at[pl.ds(z * 16, 16)], a4s, a4r, at_z(d))
            else:
                own4.append(local(Q1A.at[:, k], FA.at[pl.ds(z * 16, 16)], 10))
        own3["b", g].wait()
        wait(Q1B.at[pl.ds(0, 7), pl.ds(0, 8)], b3r.at[g])
        for k in range(4 * g, 4 * g + 4):
            dy = (k - 1) % 8
            for dc in (0, 1):
                kc = 2 * k + (c + dc) % 2
                if dy or dc:
                    send(Q1B.at[:, kc], FB.at[pl.ds(yc * 8, 8)], b4s, b4r, at_yc(dy, dc))
                else:
                    own4.append(local(Q1B.at[:, kc], FB.at[pl.ds(yc * 8, 8)], 11))

    def unpack_of(src, first_row):
        def unpack(k, carry):
            for j in range(8):
                ch = k * 8 + j
                T[pl.ds(ch + first_row, 16, stride=256), :] = src[ch].astype(F32)
            return carry

        return unpack

    for copy in own4:
        copy.wait()
    wait(FA.at[pl.ds(0, 112)], a4r)
    lax.fori_loop(0, 16, unpack_of(FA, 0), 0)
    wait(FB.at[pl.ds(0, 120)], b4r)
    lax.fori_loop(0, 16, unpack_of(FB, 128), 0)

    GA[...] = jnp.zeros_like(GA)

    def gram_term(t, carry):
        m = T[pl.ds(pl.multiple_of(t * 256, 256), 256), :].astype(BF16)
        MB[t] = m
        GA[...] += lax.dot_general(m, m, NT, preferred_element_type=F32)
        return carry

    lax.fori_loop(0, 16, gram_term, 0)

    left = GA[0:64, 0:128] + GA[128:192, 128:256]
    right = GA[64:128, 0:128] + GA[192:256, 128:256]
    g64 = left + pltpu.roll(right, 64, 1)
    low = iota((32, 128), 1) < 64
    g_part[...] = jnp.where(low, g64[0:32], pltpu.roll(g64[32:64], 64, 1))
    other_core = {"C": 1 - c}
    send(g_part.at[pl.ds((1 - c) * 16, 16)], g_core, gs.at[0], gr.at[0], other_core)
    wait(g_core, gr.at[0])
    g_z[z] = g_part[pl.ds(pl.multiple_of(c * 16, 16), 16), :] + g_core[...]
    for d in z_offsets:
        send(g_z.at[z], g_z.at[z], gs.at[1], gr.at[1], at_z(d))

    eye_cells = identity(128)

    def to_cells(t, carry):
        cells = lax.dot_general(eye_cells, MB[t], NT, preferred_element_type=F32)
        out[pl.ds(t * 2, 2)] = cells.astype(BF16).reshape(2, 64, 256)
        return carry

    lax.fori_loop(0, 16, to_cells, 0)

    wait(g_z.at[pl.ds(0, 7)], gr.at[1])
    total = g_z[0]
    for k in range(1, NZ):
        total = total + g_z[k]
    g_y[y] = total
    for d in (1, 7, 2, 6, 3, 5, 4):
        send(g_y.at[y], g_y.at[y], gs.at[2], gr.at[2], at_yc(d, 0))
    wait(g_y.at[pl.ds(0, 7)], gr.at[2])
    total = g_y[0]
    for k in range(1, NY):
        total = total + g_y[k]
    g_x[x] = total
    for d in (1, 2, 3):
        send(g_x.at[x], g_x.at[x], gs.at[3], gr.at[3], {"X": (x + d) % NX})
    wait(g_x.at[pl.ds(0, 3)], gr.at[3])
    total = g_x[0]
    for k in range(1, NX):
        total = total + g_x[k]
    g_end[c] = total * (1.0 / (4 * 2048 * 512))
    send(g_end.at[c], g_end.at[c], gs.at[4], gr.at[4], other_core)
    wait(g_end.at[0], gr.at[4])
    gram[0:16, :] = g_end[0, :, 0:64]
    gram[16:32, :] = g_end[1, :, 0:64]
    gram[32:48, :] = pltpu.roll(g_end[0], 64, 1)[:, 0:64]
    gram[48:64, :] = pltpu.roll(g_end[1], 64, 1)[:, 0:64]

    wait(SA.at[pl.ds(0, 112)], a1s)
    wait(SB.at[pl.ds(0, 120)], b1s)
    wait(R2A.at[pl.ds(0, 15)], a2s)
    wait(R2B.at[pl.ds(0, 7)], b2s)
    wait(HA, hs.at[0])
    wait(HB, hs.at[1])
    wait(OA.at[pl.ds(0, 15)], a3s)
    wait(OB.at[pl.ds(0, 7)], b3s)
    wait(FA.at[pl.ds(0, 112)], a4s)
    wait(FB.at[pl.ds(0, 120)], b4s)
    wait(g_core, gs.at[0])
    wait(g_z.at[pl.ds(0, 7)], gs.at[1])
    wait(g_y.at[pl.ds(0, 7)], gs.at[2])
    wait(g_x.at[pl.ds(0, 3)], gs.at[3])
    wait(g_end.at[0], gs.at[4])


def tiles(*lead):
    return pltpu.VMEM(lead + (ROWS, LANES), BF16)


def shards(fields):
    vmem, dma = pltpu.VMEM, pltpu.SemaphoreType.DMA
    scratch = [
        vmem((4096, 128), F32),
        tiles(128), tiles(128),
        tiles(8, 16), tiles(16, 8),
        tiles(16, 8), tiles(8, 16),
        tiles(2, 4, 8), tiles(2, 4, 8),
        vmem((256, 1024), BF16), vmem((128, 1024), BF16), vmem((256, 1024), BF16),
        vmem((768, 256), BF16), vmem((768, 128), BF16), vmem((3, 256, 256), BF16),
        tiles(16, 8), tiles(8, 16),
        tiles(16, 8), tiles(8, 16),
        tiles(128), tiles(128),
        vmem((16, 256, 128), BF16), vmem((256, 256), F32),
        vmem((32, 128), F32), vmem((16, 128), F32),
        vmem((8, 16, 128), F32), vmem((8, 16, 128), F32), vmem((4, 16, 128), F32), vmem((2, 16, 128), F32),
        dma((12,)),
        dma(()), dma(()), dma((2,)), dma((2,)),
        dma(()), dma(()), dma((2,)), dma((2,)),
        dma((2,)), dma((2,)),
        dma(()), dma(()), dma((2,)), dma((2,)),
        dma(()), dma(()), dma(()), dma(()),
        dma((5,)), dma((5,)),
    ]
    return pl.pallas_call(
        kernel,
        name="coarse_grain",
        out_shape=(
            jax.ShapeDtypeStruct((32, 64, 256), BF16),
            jax.ShapeDtypeStruct((64, 64), F32),
        ),
        in_specs=[pl.BlockSpec(memory_space=pltpu.VMEM)],
        out_specs=(pl.BlockSpec(memory_space=pltpu.VMEM), pl.BlockSpec(memory_space=pltpu.VMEM)),
        scratch_shapes=scratch,
        compiler_params=pltpu.CompilerParams(
            collective_id=0, has_side_effects=True, vmem_limit_bytes=40 << 20
        ),
    )(fields)


def solution(mesh):
    split = Mesh(mesh.devices.reshape(4, 2, 8, 4, 2), AXES)
    return jax.shard_map(
        shards, mesh=split, in_specs=(P(LON, LAT, None),), out_specs=(P(LON, LAT, None), P()), check_vma=False
    )
```

```python
import numpy as np
import jax
import jax.numpy as jnp
from jax import lax
from jax.experimental import pallas as pl
from jax.experimental.pallas import tpu as pltpu
from jax.sharding import Mesh
from jax.sharding import PartitionSpec as P

AXES = ("X", "H", "Z", "L", "C")
LON = ("X", "H", "Z")
LAT = ("L", "C")
R = 128
NX, NY, NZ = 4, 8, 8
ROWS, LANES = 16, 128
MESH_ID = pl.DeviceIdType.MESH
F32, BF16 = jnp.float32, jnp.bfloat16
NT = (((1,), (1,)), ((), ()))


def taps(distance):
    weight = jnp.exp(-((distance.astype(F32) / R) ** 2))
    return jnp.where(jnp.abs(distance) <= R, weight, 0.0)


def lon_norm():
    d = np.arange(-R, R + 1).astype(np.float32)
    return float(np.sum(np.exp(-((d / R) ** 2)).astype(BF16).astype(np.float32)))


def iota(shape, axis):
    return lax.broadcasted_iota(jnp.int32, shape, axis)


def kernel(
    fields, out, gram,
    FV, T, SA, SB, R1A, R1B, R2A, R2B, HA, HB, XA, XB, XH, SM, AO, AH, W, OA, OB, Q1A, Q1B, FA, FB, MW, GA,
    g_part, g_core, g_z, g_y, g_x,
    ins, loc, a1s, b1s, a1r, b1r, a2s, b2s, a2r, b2r, hs, hr, a3s, b3s, a3r, b3r, a4s, b4s, a4r, b4r, gs, gr,
):
    x, h, z = lax.axis_index("X"), lax.axis_index("H"), lax.axis_index("Z")
    l, c = lax.axis_index("L"), lax.axis_index("C")
    y = h * 4 + l
    yc = y * 2 + c

    def at_z(d):
        return {"Z": (z + d) % NZ}

    def at_yc(dy, dc):
        yy = (y + dy) % NY
        return {"H": yy // 4, "L": yy % 4, "C": (c + dc) % 2}

    def at_xc(dx, dc):
        return {"X": (x + dx) % NX, "C": (c + dc) % 2}

    def send(src, dst, ssem, rsem, device):
        pltpu.make_async_remote_copy(src, dst, ssem, rsem, device_id=device, device_id_type=MESH_ID).start()

    def wait(ref, sem):
        pltpu.make_async_copy(ref, ref, sem).wait()

    def local(src, dst, k):
        copy = pltpu.make_async_copy(src, dst, loc.at[k])
        copy.start()
        return copy

    z_near = [1, 7, 6, 5, 4, 3, 2]
    z_far = [4, 3, 5, 2, 6, 1, 7]
    yc_near = [(dy, dc) for dy in (1, 7, 6, 5, 4, 3, 2, 0) for dc in (0, 1) if (dy, dc) != (0, 0)]
    yc_far = [(dy, dc) for dy in (4, 3, 5, 2, 6, 1, 7, 0) for dc in (0, 1) if (dy, dc) != (0, 0)]
    xc_far = [(2, 0), (2, 1), (1, 0), (3, 0), (1, 1), (3, 1), (0, 1)]

    pieces = []
    for k in range(4):
        pieces.append(pltpu.make_async_copy(fields.at[pl.ds(8 * k, 8)], FV.at[pl.ds(8 * k, 8)], ins.at[k]))
        pieces[k].start()

    barrier = pltpu.get_barrier_semaphore()
    for d in z_far:
        pl.semaphore_signal(barrier, inc=1, device_id=at_z(d), device_id_type=MESH_ID)
    for dy, dc in yc_far:
        pl.semaphore_signal(barrier, inc=1, device_id=at_yc(dy, dc), device_id_type=MESH_ID)
    for dx, dc in xc_far[:6]:
        pl.semaphore_signal(barrier, inc=1, device_id=at_xc(dx, dc), device_id_type=MESH_ID)

    def to_channels(t, carry):
        f = jnp.transpose(FV[pl.ds(t * 2, 2)].reshape(128, 256)).astype(F32)
        u, v, w, b = f[0:64], f[64:128], f[128:192], f[192:256]
        base = pl.multiple_of(t * 256, 256)
        T[pl.ds(base, 64), :] = u * b
        T[pl.ds(base + 64, 64), :] = v * b
        T[pl.ds(base + 128, 64), :] = w * b
        T[pl.ds(base + 192, 64), :] = u * v
        return carry

    for k in range(4):
        pieces[k].wait()
        lax.fori_loop(4 * k, 4 * k + 4, to_channels, 0, unroll=4)

    def pack_of(dst, first_row):
        def pack(k, carry):
            for j in range(8):
                ch = k * 8 + j
                dst[ch] = T[pl.ds(ch + first_row, 16, stride=256), :].astype(BF16)
            return carry

        return pack

    lax.fori_loop(0, 16, pack_of(SA, 0), 0)
    pl.semaphore_wait(barrier, 28)
    for d in z_near:
        i = (1 - d) % 8
        send(SA.at[pl.ds(((z + d) % NZ) * 16, 16)], R1A.at[i], a1s, a1r.at[i // 4], at_z(d))
    own_a1 = local(SA.at[pl.ds(z * 16, 16)], R1A.at[1], 0)
    lax.fori_loop(0, 16, pack_of(SB, 128), 0)
    for dy, dc in yc_near:
        i = (1 - dy) % 8
        to = ((y + dy) % NY) * 2 + (c + dc) % 2
        send(SB.at[pl.ds(to * 8, 8)], R1B.at[2 * i + c], b1s, b1r.at[i // 4], at_yc(dy, dc))
    own_b1 = local(SB.at[pl.ds(yc * 8, 8)], R1B.at[2 + c], 1)

    def lon_matrix(k, carry):
        edge = k // 4
        for block, shift in ((0, 0), (1, -1), (2, 1)):
            row = iota((32, 256), 0) + (k % 4) * 32
            row = row + (1 - edge) * 64 + edge * 128 * (row // 64)
            base = pl.multiple_of(edge * 384 + block * 128 + (k % 4) * 32, 32)
            AO[pl.ds(base, 32), :] = taps(2 * (iota((32, 256), 1) - row) + shift).astype(BF16)
        return carry

    lax.fori_loop(0, 8, lon_matrix, 0)

    def halo_matrix(k, carry):
        for block, shift in ((0, 0), (1, -1), (2, 1)):
            row = iota((32, 128), 0) + k * 32
            row = row + 128 * (row // 64)
            col = iota((32, 128), 1)
            col = jnp.where(col < 64, col - 64, col + 192)
            base = pl.multiple_of(block * 128 + k * 32, 32)
            AH[pl.ds(base, 32), :] = taps(2 * (col - row) + shift).astype(BF16)
        return carry

    lax.fori_loop(0, 4, halo_matrix, 0)

    def lat_matrix(k, carry):
        src = iota((32, 256), 0) + k * 32
        dst = iota((32, 256), 1)
        same = (src // 64) % 2 == (dst // 64) % 2
        apart = 64 * (src // 128 - dst // 128) + src % 64 - dst % 64
        for step in range(3):
            W[step, pl.ds(k * 32, 32), :] = jnp.where(same, taps(apart - 128 * (step - 1)), 0.0).astype(BF16)
        return carry

    lax.fori_loop(0, 8, lat_matrix, 0)
    ones = jnp.ones((16, 256), BF16)
    lat_sums = [jnp.dot(ones, W[k], preferred_element_type=F32)[0:1] for k in range(3)]
    inv_lat = []
    for dst in range(4):
        total = lat_sums[1]
        if dst > 0:
            total = total + lat_sums[2]
        if dst < 3:
            total = total + lat_sums[0]
        inv_lat.append(1.0 / total)
    inv_lon = 1.0 / lon_norm()

    own2 = []
    for g in (0, 1):
        if g == 0:
            own_a1.wait()
            wait(R1A.at[pl.ds(0, 3)], a1r.at[0])
        else:
            wait(R1A.at[pl.ds(0, 4)], a1r.at[1])
        for dy, dc in yc_far:
            to = ((y + dy) % NY) * 2 + (c + dc) % 2
            send(R1A.at[pl.ds(4 * g, 4), to], R2A.at[yc, pl.ds(4 * g, 4)], a2s, a2r.at[g], at_yc(dy, dc))
        own2.append(local(R1A.at[pl.ds(4 * g, 4), yc], R2A.at[yc, pl.ds(4 * g, 4)], 2 + g))
        if g == 0:
            own_b1.wait()
            wait(R1B.at[pl.ds(0, 7)], b1r.at[0])
        else:
            wait(R1B.at[pl.ds(0, 8)], b1r.at[1])
        for d in z_far:
            send(R1B.at[pl.ds(8 * g, 8), (z + d) % NZ], R2B.at[z, pl.ds(8 * g, 8)], b2s, b2r.at[g], at_z(d))
        own2.append(local(R1B.at[pl.ds(8 * g, 8), z], R2B.at[z, pl.ds(8 * g, 8)], 4 + g))

    def halo_a(g):
        own2[2 * g].wait()
        wait(R2A.at[pl.ds(0, 15), pl.ds(0, 4)], a2r.at[g])
        for i in range(4 * g, 4 * g + 4):
            zz = (z + i + 7) % NZ
            hi = zz // 4
            send(R2A.at[pl.ds(hi * 8, 8), i], HA.at[hi, zz % 4], hs.at[0], hr.at[0], at_xc(2 * hi + 3, 0))

    def halo_b(g):
        own2[2 * g + 1].wait()
        wait(R2B.at[pl.ds(0, 7), pl.ds(0, 8)], b2r.at[g])
        for i in range(4 * g, 4 * g + 4):
            yy = (y + i + 7) % NY
            hi = yy // 4
            send(
                R2B.at[pl.ds(hi * 4, 4), pl.ds(2 * i, 2)],
                HB.at[hi, :, pl.ds((yy % 4) * 2, 2)],
                hs.at[1], hr.at[1], at_xc(2 * hi + 3, 0),
            )

    def gather(tile_of, X):
        def rows(lam, carry):
            for mu in range(8):
                X[pl.ds(pl.multiple_of(lam * 16, 16), 16), mu * 128 : mu * 128 + 128] = tile_of(lam, mu)
            return carry

        lax.fori_loop(0, 16, rows, 0)

    def gather_halo(halo):
        for hi in (0, 1):
            for zz in range(4):
                for mu in range(8):
                    row = (1 - hi) * 64 + zz * 16
                    XH[row : row + 16, mu * 128 : mu * 128 + 128] = halo[hi, zz, mu]

    def filtered(X, edge, store):
        first = iota((128, 128), 1) < 64
        lams = [0, 1, 2, 3, 12, 13, 14, 15] if edge else list(range(4, 12))
        for n in range(4):
            cols = slice(n * 256, n * 256 + 256)
            zs = jnp.dot(AO[edge * 384 : edge * 384 + 384], X[:, cols], preferred_element_type=F32)
            if edge:
                zs = zs + jnp.dot(AH[...], XH[:, cols], preferred_element_type=F32)
            for half in range(2):
                part = zs[:, half * 128 : half * 128 + 128]
                other = jnp.where(first, part[128:256], part[256:384])
                total = part[0:128] + pltpu.roll(other, 64, 1)
                at = n * 256 + half * 128
                SM[:, at : at + 128] = (total * inv_lon).astype(BF16)
        for dst in range(4):
            total = None
            for src in range(max(0, dst - 1), min(3, dst + 1) + 1):
                term = jnp.dot(SM[:, src * 256 : src * 256 + 256], W[dst - src + 1], preferred_element_type=F32)
                total = term if total is None else total + term
            total = (total * inv_lat[dst]).astype(BF16)
            for k, lam in enumerate(lams):
                for half in range(2):
                    store(lam, 2 * dst + half, total[k * 16 : k * 16 + 16, half * 128 : half * 128 + 128])

    def store_a(lam, mu, tile):
        OA[(lam // 8) * 8 + mu, lam % 8] = tile

    def store_b(lam, mu, tile):
        OB[lam % 8, (lam // 8) * 8 + mu] = tile

    def send_a(edge):
        for dy, dc in yc_far:
            yy = (y + dy) % NY
            to = yy * 2 + (c + dc) % 2
            at = 4 * (yy // 4) if edge else 4 - 4 * (yy // 4)
            send(OA.at[to, pl.ds(at, 4)], Q1A.at[yc, pl.ds(at, 4)], a3s, a3r.at[edge], at_yc(dy, dc))
        at = 4 * h if edge else 4 - 4 * h
        return local(OA.at[yc, pl.ds(at, 4)], Q1A.at[yc, pl.ds(at, 4)], 6 + edge)

    def send_b(edge):
        for d in z_far:
            zz = (z + d) % NZ
            at = 8 * (zz // 4) if edge else 8 - 8 * (zz // 4)
            send(OB.at[zz, pl.ds(at, 8)], Q1B.at[z, pl.ds(at, 8)], b3s, b3r.at[edge], at_z(d))
        at = 8 * (z // 4) if edge else 8 - 8 * (z // 4)
        return local(OB.at[z, pl.ds(at, 8)], Q1B.at[z, pl.ds(at, 8)], 8 + edge)

    halo_a(0)
    halo_b(0)
    halo_a(1)
    gather(lambda lam, mu: R2A[(lam // 8) * 8 + mu, (lam % 8 - z + 9) % NZ], XA)
    filtered(XA, 0, store_a)
    own3 = [send_a(0)]
    halo_b(1)
    gather(lambda lam, mu: R2B[lam % 8, 2 * (((lam // 8) * 4 + mu // 2 - y + 9) % NY) + mu % 2], XB)
    filtered(XB, 0, store_b)
    own3.append(send_b(0))
    wait(HA, hr.at[0])
    gather_halo(HA)
    filtered(XA, 1, store_a)
    own3.append(send_a(1))
    wait(HB, hr.at[1])
    gather_halo(HB)
    filtered(XB, 1, store_b)
    own3.append(send_b(1))

    own3[0].wait()
    own3[2].wait()
    for edge in (0, 1):
        wait(Q1A.at[pl.ds(0, 15), pl.ds(0, 4)], a3r.at[edge])
    for d in z_far:
        send(Q1A.at[:, (z + d) % NZ], FA.at[pl.ds(z * 16, 16)], a4s, a4r, at_z(d))
    own_a4 = local(Q1A.at[:, z], FA.at[pl.ds(z * 16, 16)], 10)
    own3[1].wait()
    own3[3].wait()
    for edge in (0, 1):
        wait(Q1B.at[pl.ds(0, 7), pl.ds(0, 8)], b3r.at[edge])
    for dy, dc in yc_far:
        to = ((y + dy) % NY) * 2 + (c + dc) % 2
        send(Q1B.at[:, to], FB.at[pl.ds(yc * 8, 8)], b4s, b4r, at_yc(dy, dc))
    own_b4 = local(Q1B.at[:, yc], FB.at[pl.ds(yc * 8, 8)], 11)

    def home(src, first_row):
        def unpack(k, carry):
            for j in range(8):
                ch = k * 8 + j
                T[pl.ds(ch + first_row, 16, stride=256), :] = src[ch].astype(F32)
            return carry

        lax.fori_loop(0, 16, unpack, 0)
        rows = slice(first_row, first_row + 128)
        for t in range(16):
            at = t * 256 + first_row
            MW[rows, t * 128 : t * 128 + 128] = T[at : at + 128, :].astype(BF16)
        GA[rows] = lax.dot_general(MW[rows], MW[rows], NT, preferred_element_type=F32)

    own_a4.wait()
    wait(FA.at[pl.ds(0, 112)], a4r)
    home(FA, 0)
    own_b4.wait()
    wait(FB.at[pl.ds(0, 120)], b4r)
    home(FB, 128)

    left = GA[0:64] + GA[128:192]
    right = GA[64:128] + GA[192:256]
    g64 = left + pltpu.roll(right, 64, 1)
    low = iota((32, 128), 1) < 64
    g_part[...] = jnp.where(low, g64[0:32], pltpu.roll(g64[32:64], 64, 1))
    send(g_part.at[pl.ds((1 - c) * 16, 16)], g_core, gs.at[0], gr.at[0], at_yc(0, 1))
    wait(g_core, gr.at[0])
    g_z[z] = g_part[pl.ds(pl.multiple_of(c * 16, 16), 16), :] + g_core[...]
    for d in z_far:
        send(g_z.at[z], g_z.at[z], gs.at[1], gr.at[1], at_z(d))

    def to_cells(t, carry):
        cells = jnp.transpose(MW[:, pl.ds(pl.multiple_of(t * 128, 128), 128)])
        FV[pl.ds(t * 2, 2)] = cells.reshape(2, 64, 256)
        return carry

    lax.fori_loop(0, 16, to_cells, 0, unroll=4)
    finished = pltpu.make_async_copy(FV, out, ins.at[0])
    finished.start()

    wait(g_z.at[pl.ds(0, 7)], gr.at[1])
    total = g_z[0]
    for k in range(1, NZ):
        total = total + g_z[k]
    g_y[y] = total
    for d in z_far:
        send(g_y.at[y], g_y.at[y], gs.at[2], gr.at[2], at_yc(d, 0))
    wait(g_y.at[pl.ds(0, 7)], gr.at[2])
    total = g_y[0]
    for k in range(1, NY):
        total = total + g_y[k]
    g_x[c, x] = total * (1.0 / (4 * 2048 * 512))
    for dx, dc in xc_far:
        send(g_x.at[c, x], g_x.at[c, x], gs.at[3], gr.at[3], at_xc(dx, dc))
    wait(g_y.at[pl.ds(0, 7)], gr.at[3])
    for half in range(2):
        total = g_x[half, 0]
        for k in range(1, NX):
            total = total + g_x[half, k]
        gram[half * 16 : half * 16 + 16, :] = total[:, 0:64]
        gram[32 + half * 16 : 48 + half * 16, :] = pltpu.roll(total, 64, 1)[:, 0:64]

    finished.wait()
    wait(SA.at[pl.ds(0, 112)], a1s)
    wait(SB.at[pl.ds(0, 120)], b1s)
    wait(R2A.at[pl.ds(0, 15)], a2s)
    wait(R2B.at[pl.ds(0, 7)], b2s)
    wait(HA, hs.at[0])
    wait(HB, hs.at[1])
    wait(OA.at[pl.ds(0, 15)], a3s)
    wait(OB.at[pl.ds(0, 7)], b3s)
    wait(FA.at[pl.ds(0, 112)], a4s)
    wait(FB.at[pl.ds(0, 120)], b4s)
    wait(g_core, gs.at[0])
    for k in (1, 2, 3):
        wait(g_z.at[pl.ds(0, 7)], gs.at[k])


def tiles(*lead):
    return pltpu.VMEM(lead + (ROWS, LANES), BF16)


def shards(fields):
    vmem, dma = pltpu.VMEM, pltpu.SemaphoreType.DMA
    scratch = [
        vmem((32, 64, 256), BF16),
        vmem((4096, 128), F32),
        tiles(128), tiles(128),
        tiles(8, 16), tiles(16, 8),
        tiles(16, 8), tiles(8, 16),
        tiles(2, 4, 8), tiles(2, 4, 8),
        vmem((256, 1024), BF16), vmem((256, 1024), BF16), vmem((128, 1024), BF16), vmem((128, 1024), BF16),
        vmem((768, 256), BF16), vmem((384, 128), BF16), vmem((3, 256, 256), BF16),
        tiles(16, 8), tiles(8, 16),
        tiles(16, 8), tiles(8, 16),
        tiles(128), tiles(128),
        vmem((256, 2048), BF16), vmem((256, 128), F32),
        vmem((32, 128), F32), vmem((16, 128), F32),
        vmem((8, 16, 128), F32), vmem((8, 16, 128), F32), vmem((2, 4, 16, 128), F32),
        dma((4,)), dma((12,)),
        dma(()), dma(()), dma((2,)), dma((2,)),
        dma(()), dma(()), dma((2,)), dma((2,)),
        dma((2,)), dma((2,)),
        dma(()), dma(()), dma((2,)), dma((2,)),
        dma(()), dma(()), dma(()), dma(()),
        dma((4,)), dma((4,)),
    ]
    return pl.pallas_call(
        kernel,
        name="coarse_grain",
        out_shape=(
            jax.ShapeDtypeStruct((32, 64, 256), BF16),
            jax.ShapeDtypeStruct((64, 64), F32),
        ),
        in_specs=[pl.BlockSpec(memory_space=pltpu.HBM)],
        out_specs=(pl.BlockSpec(memory_space=pltpu.HBM), pl.BlockSpec(memory_space=pltpu.VMEM)),
        scratch_shapes=scratch,
        compiler_params=pltpu.CompilerParams(
            collective_id=0, has_side_effects=True, vmem_limit_bytes=56_000_000
        ),
    )(fields)


def solution(mesh):
    split = Mesh(mesh.devices.reshape(4, 2, 8, 4, 2), AXES)
    return jax.shard_map(
        shards, mesh=split, in_specs=(P(LON, LAT, None),), out_specs=(P(LON, LAT, None), P()), check_vma=False
    )
```

```python
import numpy as np
import jax
import jax.numpy as jnp
from jax import lax
from jax.experimental import pallas as pl
from jax.experimental.pallas import tpu as pltpu
from jax.sharding import Mesh
from jax.sharding import PartitionSpec as P

AXES = ("X", "H", "Z", "L", "C")
LON = ("X", "H", "Z")
LAT = ("L", "C")
R = 128
NX, NY, NZ = 4, 8, 8
ROWS, LANES = 16, 128
MESH_ID = pl.DeviceIdType.MESH
F32, BF16 = jnp.float32, jnp.bfloat16
NT = (((1,), (1,)), ((), ()))


def taps(distance):
    weight = jnp.exp(-((distance.astype(F32) / R) ** 2))
    return jnp.where(jnp.abs(distance) <= R, weight, 0.0)


def lon_norm():
    d = np.arange(-R, R + 1).astype(np.float32)
    return float(np.sum(np.exp(-((d / R) ** 2)).astype(BF16).astype(np.float32)))


def iota(shape, axis):
    return lax.broadcasted_iota(jnp.int32, shape, axis)


def kernel(
    fields, out, gram,
    FV, T, SA, SB, R1A, R1B, R2A, R2B, HA, HB, XA, XB, XH, SM, AO, AH, W, OA, OB, Q1A, Q1B, FA, FB, MW, GA,
    g_part, g_core, g_z, g_y, g_x,
    ins, loc, a1s, b1s, a1r, b1r, a2s, b2s, a2r, b2r, hs, hr, a3s, b3s, a3r, b3r, a4s, b4s, a4r, b4r, gs, gr,
):
    x, h, z = lax.axis_index("X"), lax.axis_index("H"), lax.axis_index("Z")
    l, c = lax.axis_index("L"), lax.axis_index("C")
    y = h * 4 + l
    yc = y * 2 + c

    def at_z(d):
        return {"Z": (z + d) % NZ}

    def at_yc(dy, dc):
        yy = (y + dy) % NY
        return {"H": yy // 4, "L": yy % 4, "C": (c + dc) % 2}

    def at_xc(dx, dc):
        return {"X": (x + dx) % NX, "C": (c + dc) % 2}

    def send(src, dst, ssem, rsem, device):
        pltpu.make_async_remote_copy(src, dst, ssem, rsem, device_id=device, device_id_type=MESH_ID).start()

    def wait(ref, sem):
        pltpu.make_async_copy(ref, ref, sem).wait()

    def local(src, dst, k):
        copy = pltpu.make_async_copy(src, dst, loc.at[k])
        copy.start()
        return copy

    z_near = [1, 7, 6, 5, 4, 3, 2]
    z_far = [4, 3, 5, 2, 6, 1, 7]
    yc_near = [(dy, dc) for dy in (1, 7, 6, 5, 4, 3, 2, 0) for dc in (0, 1) if (dy, dc) != (0, 0)]
    yc_far = [(dy, dc) for dy in (4, 3, 5, 2, 6, 1, 7, 0) for dc in (0, 1) if (dy, dc) != (0, 0)]
    xc_far = [(2, 0), (2, 1), (1, 0), (3, 0), (1, 1), (3, 1), (0, 1)]

    pieces = []
    for k in range(4):
        pieces.append(pltpu.make_async_copy(fields.at[pl.ds(8 * k, 8)], FV.at[pl.ds(8 * k, 8)], ins.at[k]))
        pieces[k].start()

    barrier = pltpu.get_barrier_semaphore()
    for d in z_far:
        pl.semaphore_signal(barrier, inc=1, device_id=at_z(d), device_id_type=MESH_ID)
    for dy, dc in yc_far:
        pl.semaphore_signal(barrier, inc=1, device_id=at_yc(dy, dc), device_id_type=MESH_ID)
    for dx, dc in xc_far[:6]:
        pl.semaphore_signal(barrier, inc=1, device_id=at_xc(dx, dc), device_id_type=MESH_ID)

    def to_channels(t, carry):
        f = jnp.transpose(FV[pl.ds(t * 2, 2)].reshape(128, 256)).astype(F32)
        u, v, w, b = f[0:64], f[64:128], f[128:192], f[192:256]
        base = pl.multiple_of(t * 256, 256)
        T[pl.ds(base, 64), :] = u * b
        T[pl.ds(base + 64, 64), :] = v * b
        T[pl.ds(base + 128, 64), :] = w * b
        T[pl.ds(base + 192, 64), :] = u * v
        return carry

    for k in range(4):
        pieces[k].wait()
        lax.fori_loop(4 * k, 4 * k + 4, to_channels, 0, unroll=4)

    def pack_of(dst, first_row):
        def pack(k, carry):
            for j in range(8):
                ch = k * 8 + j
                dst[ch] = T[pl.ds(ch + first_row, 16, stride=256), :].astype(BF16)
            return carry

        return pack

    lax.fori_loop(0, 16, pack_of(SA, 0), 0)
    pl.semaphore_wait(barrier, 28)
    for d in z_near:
        i = (1 - d) % 8
        send(SA.at[pl.ds(((z + d) % NZ) * 16, 16)], R1A.at[i], a1s, a1r.at[i // 4], at_z(d))
    own_a1 = local(SA.at[pl.ds(z * 16, 16)], R1A.at[1], 0)
    lax.fori_loop(0, 16, pack_of(SB, 128), 0)
    for dy, dc in yc_near:
        i = (1 - dy) % 8
        to = ((y + dy) % NY) * 2 + (c + dc) % 2
        send(SB.at[pl.ds(to * 8, 8)], R1B.at[2 * i + c], b1s, b1r.at[i // 4], at_yc(dy, dc))
    own_b1 = local(SB.at[pl.ds(yc * 8, 8)], R1B.at[2 + c], 1)

    def lon_matrix(k, carry):
        edge = k // 4
        for block, shift in ((0, 0), (1, -1), (2, 1)):
            row = iota((32, 256), 0) + (k % 4) * 32
            row = row + (1 - edge) * 64 + edge * 128 * (row // 64)
            base = pl.multiple_of(edge * 384 + block * 128 + (k % 4) * 32, 32)
            AO[pl.ds(base, 32), :] = taps(2 * (iota((32, 256), 1) - row) + shift).astype(BF16)
        return carry

    lax.fori_loop(0, 8, lon_matrix, 0)

    def halo_matrix(k, carry):
        for block, shift in ((0, 0), (1, -1), (2, 1)):
            row = iota((32, 128), 0) + k * 32
            row = row + 128 * (row // 64)
            col = iota((32, 128), 1)
            col = jnp.where(col < 64, col - 64, col + 192)
            base = pl.multiple_of(block * 128 + k * 32, 32)
            AH[pl.ds(base, 32), :] = taps(2 * (col - row) + shift).astype(BF16)
        return carry

    lax.fori_loop(0, 4, halo_matrix, 0)

    def lat_matrix(k, carry):
        src = iota((32, 256), 0) + k * 32
        dst = iota((32, 256), 1)
        same = (src // 64) % 2 == (dst // 64) % 2
        apart = 64 * (src // 128 - dst // 128) + src % 64 - dst % 64
        for step in range(3):
            W[step, pl.ds(k * 32, 32), :] = jnp.where(same, taps(apart - 128 * (step - 1)), 0.0).astype(BF16)
        return carry

    lax.fori_loop(0, 8, lat_matrix, 0)
    ones = jnp.ones((16, 256), BF16)
    lat_sums = [jnp.dot(ones, W[k], preferred_element_type=F32)[0:1] for k in range(3)]
    inv_lat = []
    for dst in range(4):
        total = lat_sums[1]
        if dst > 0:
            total = total + lat_sums[2]
        if dst < 3:
            total = total + lat_sums[0]
        inv_lat.append(1.0 / total)
    inv_lon = 1.0 / lon_norm()

    own2 = []
    for g in (0, 1):
        if g == 0:
            own_a1.wait()
            wait(R1A.at[pl.ds(0, 3)], a1r.at[0])
        else:
            wait(R1A.at[pl.ds(0, 4)], a1r.at[1])
        for dy, dc in yc_far:
            to = ((y + dy) % NY) * 2 + (c + dc) % 2
            send(R1A.at[pl.ds(4 * g, 4), to], R2A.at[yc, pl.ds(4 * g, 4)], a2s, a2r.at[g], at_yc(dy, dc))
        own2.append(local(R1A.at[pl.ds(4 * g, 4), yc], R2A.at[yc, pl.ds(4 * g, 4)], 2 + g))
        if g == 0:
            own_b1.wait()
            wait(R1B.at[pl.ds(0, 7)], b1r.at[0])
        else:
            wait(R1B.at[pl.ds(0, 8)], b1r.at[1])
        for d in z_far:
            send(R1B.at[pl.ds(8 * g, 8), (z + d) % NZ], R2B.at[z, pl.ds(8 * g, 8)], b2s, b2r.at[g], at_z(d))
        own2.append(local(R1B.at[pl.ds(8 * g, 8), z], R2B.at[z, pl.ds(8 * g, 8)], 4 + g))

    def halo_a(g):
        own2[2 * g].wait()
        wait(R2A.at[pl.ds(0, 15), pl.ds(0, 4)], a2r.at[g])
        for i in range(4 * g, 4 * g + 4):
            zz = (z + i + 7) % NZ
            hi = zz // 4
            send(R2A.at[pl.ds(hi * 8, 8), i], HA.at[hi, zz % 4], hs.at[0], hr.at[0], at_xc(2 * hi + 3, 0))

    def halo_b(g):
        own2[2 * g + 1].wait()
        wait(R2B.at[pl.ds(0, 7), pl.ds(0, 8)], b2r.at[g])
        for i in range(4 * g, 4 * g + 4):
            yy = (y + i + 7) % NY
            hi = yy // 4
            send(
                R2B.at[pl.ds(hi * 4, 4), pl.ds(2 * i, 2)],
                HB.at[hi, :, pl.ds((yy % 4) * 2, 2)],
                hs.at[1], hr.at[1], at_xc(2 * hi + 3, 0),
            )

    def gather_a(g):
        for i in range(4 * g, 4 * g + 4):
            zz = (z + i + 7) % NZ
            for hh in (0, 1):
                row = pl.multiple_of((8 * hh + zz) * 16, 16)
                for mu in range(8):
                    XA[pl.ds(row, 16), mu * 128 : mu * 128 + 128] = R2A[8 * hh + mu, i]

    def gather_b(g):
        for i in range(4 * g, 4 * g + 4):
            yy = (y + i + 7) % NY
            for zz in range(8):
                row = pl.multiple_of((8 * (yy // 4) + zz) * 16, 16)
                for core in (0, 1):
                    col = pl.multiple_of((2 * (yy % 4) + core) * 128, 128)
                    XB[pl.ds(row, 16), pl.ds(col, 128)] = R2B[zz, 2 * i + core]

    def gather_halo(halo):
        for hi in (0, 1):
            for zz in range(4):
                for mu in range(8):
                    row = (1 - hi) * 64 + zz * 16
                    XH[row : row + 16, mu * 128 : mu * 128 + 128] = halo[hi, zz, mu]

    def filtered(X, edge, store):
        first = iota((128, 128), 1) < 64
        lams = [0, 1, 2, 3, 12, 13, 14, 15] if edge else list(range(4, 12))
        for n in range(4):
            cols = slice(n * 256, n * 256 + 256)
            zs = jnp.dot(AO[edge * 384 : edge * 384 + 384], X[:, cols], preferred_element_type=F32)
            if edge:
                zs = zs + jnp.dot(AH[...], XH[:, cols], preferred_element_type=F32)
            for half in range(2):
                part = zs[:, half * 128 : half * 128 + 128]
                other = jnp.where(first, part[128:256], part[256:384])
                total = part[0:128] + pltpu.roll(other, 64, 1)
                at = n * 256 + half * 128
                SM[:, at : at + 128] = (total * inv_lon).astype(BF16)
        for dst in range(4):
            total = None
            for src in range(max(0, dst - 1), min(3, dst + 1) + 1):
                term = jnp.dot(SM[:, src * 256 : src * 256 + 256], W[dst - src + 1], preferred_element_type=F32)
                total = term if total is None else total + term
            total = (total * inv_lat[dst]).astype(BF16)
            for k, lam in enumerate(lams):
                for half in range(2):
                    store(lam, 2 * dst + half, total[k * 16 : k * 16 + 16, half * 128 : half * 128 + 128])

    def store_a(lam, mu, tile):
        OA[(lam // 8) * 8 + mu, lam % 8] = tile

    def store_b(lam, mu, tile):
        OB[lam % 8, (lam // 8) * 8 + mu] = tile

    def part_of(high, part, unit):
        return 4 * unit * (1 - high) if part == 0 else 4 * unit * high + 2 * unit * (part - 1)

    def send_a(part):
        n = 2 if part else 4
        for dy, dc in yc_far:
            yy = (y + dy) % NY
            to = yy * 2 + (c + dc) % 2
            at = pl.ds(part_of(yy // 4, part, 1), n)
            send(OA.at[to, at], Q1A.at[yc, at], a3s, a3r.at[part], at_yc(dy, dc))
        at = pl.ds(part_of(h, part, 1), n)
        return local(OA.at[yc, at], Q1A.at[yc, at], 6 + part)

    def send_b(part):
        n = 4 if part else 8
        for d in z_far:
            zz = (z + d) % NZ
            at = pl.ds(part_of(zz // 4, part, 2), n)
            send(OB.at[zz, at], Q1B.at[z, at], b3s, b3r.at[part], at_z(d))
        at = pl.ds(part_of(z // 4, part, 2), n)
        return local(OB.at[z, at], Q1B.at[z, at], 9 + part)

    halo_a(0)
    halo_b(0)
    gather_a(0)
    gather_b(0)
    halo_a(1)
    gather_a(1)
    filtered(XA, 0, store_a)
    own3 = [send_a(0)]
    halo_b(1)
    gather_b(1)
    filtered(XB, 0, store_b)
    own3.append(send_b(0))
    wait(HA, hr.at[0])
    gather_halo(HA)
    filtered(XA, 1, store_a)
    own3.append(send_a(1))
    own3.append(send_a(2))
    wait(HB, hr.at[1])
    gather_halo(HB)
    filtered(XB, 1, store_b)
    own3.append(send_b(1))
    own3.append(send_b(2))

    for part, ka, kb in ((0, 0, 1), (1, 2, 4), (2, 3, 5)):
        n = 2 if part else 4
        own3[ka].wait()
        wait(Q1A.at[pl.ds(0, 15), pl.ds(0, n)], a3r.at[part])
        for k in range(n):
            zz = part_of(h, part, 1) + (z + k) % n

            @pl.when(zz != z)
            def _():
                there = (zz - z + NZ) % NZ
                send(Q1A.at[:, zz], FA.at[pl.ds(z * 16, 16)], a4s, a4r.at[there], {"Z": zz})

        own3[kb].wait()
        wait(Q1B.at[pl.ds(0, 7), pl.ds(0, 2 * n)], b3r.at[part])
        for k in range(n):
            yy = part_of(z // 4, part, 1) + (y + k) % n
            there = (yy - y + NY) % NY
            for dc in (1, 0):
                cc = (c + dc) % 2

                def send_home():
                    send(
                        Q1B.at[:, yy * 2 + cc], FB.at[pl.ds(yc * 8, 8)], b4s, b4r.at[there],
                        {"H": yy // 4, "L": yy % 4, "C": cc},
                    )

                if dc:
                    send_home()
                else:
                    pl.when(yy != y)(send_home)

    own_a4 = local(Q1A.at[:, z], FA.at[pl.ds(z * 16, 16)], 12)
    own_b4 = local(Q1B.at[:, yc], FB.at[pl.ds(yc * 8, 8)], 13)

    def home(src, ch, row):
        for j in range(16):
            T[pl.ds(row + j, 16, stride=256), :] = src[ch + j].astype(F32)
        row = pl.multiple_of(row, 16)
        for t in range(16):
            MW[pl.ds(row, 16), t * 128 : t * 128 + 128] = T[pl.ds(t * 256 + row, 16), :].astype(BF16)

    own_a4.wait()
    home(FA, z * 16, z * 16)
    own_b4.wait()
    wait(FB.at[pl.ds(0, 8)], b4r.at[0])
    home(FB, y * 16, 128 + y * 16)
    for d in (1, 7, 2, 6, 3, 5, 4):
        wait(FA.at[pl.ds(0, 16)], a4r.at[d])
        zz = (z - d + NZ) % NZ
        home(FA, zz * 16, zz * 16)
        wait(FB.at[pl.ds(0, 16)], b4r.at[d])
        yy = (y - d + NY) % NY
        home(FB, yy * 16, 128 + yy * 16)
    for rows in (slice(0, 128), slice(128, 256)):
        GA[rows] = lax.dot_general(MW[rows], MW[rows], NT, preferred_element_type=F32)

    left = GA[0:64] + GA[128:192]
    right = GA[64:128] + GA[192:256]
    g64 = left + pltpu.roll(right, 64, 1)
    low = iota((32, 128), 1) < 64
    g_part[...] = jnp.where(low, g64[0:32], pltpu.roll(g64[32:64], 64, 1))
    send(g_part.at[pl.ds((1 - c) * 16, 16)], g_core, gs.at[0], gr.at[0], at_yc(0, 1))
    wait(g_core, gr.at[0])
    g_z[z] = g_part[pl.ds(pl.multiple_of(c * 16, 16), 16), :] + g_core[...]
    for d in z_far:
        send(g_z.at[z], g_z.at[z], gs.at[1], gr.at[1], at_z(d))

    def to_cells(t, carry):
        cells = jnp.transpose(MW[:, pl.ds(pl.multiple_of(t * 128, 128), 128)])
        out[pl.ds(t * 2, 2)] = cells.reshape(2, 64, 256)
        return carry

    lax.fori_loop(0, 16, to_cells, 0, unroll=4)

    wait(g_z.at[pl.ds(0, 7)], gr.at[1])
    total = g_z[0]
    for k in range(1, NZ):
        total = total + g_z[k]
    g_y[y] = total
    for d in z_far:
        send(g_y.at[y], g_y.at[y], gs.at[2], gr.at[2], at_yc(d, 0))
    wait(g_y.at[pl.ds(0, 7)], gr.at[2])
    total = g_y[0]
    for k in range(1, NY):
        total = total + g_y[k]
    g_x[c, x] = total * (1.0 / (4 * 2048 * 512))
    for dx, dc in xc_far:
        send(g_x.at[c, x], g_x.at[c, x], gs.at[3], gr.at[3], at_xc(dx, dc))
    wait(g_y.at[pl.ds(0, 7)], gr.at[3])
    for half in range(2):
        total = g_x[half, 0]
        for k in range(1, NX):
            total = total + g_x[half, k]
        gram[half * 16 : half * 16 + 16, :] = total[:, 0:64]
        gram[32 + half * 16 : 48 + half * 16, :] = pltpu.roll(total, 64, 1)[:, 0:64]

    wait(SA.at[pl.ds(0, 112)], a1s)
    wait(SB.at[pl.ds(0, 120)], b1s)
    wait(R2A.at[pl.ds(0, 15)], a2s)
    wait(R2B.at[pl.ds(0, 7)], b2s)
    wait(HA, hs.at[0])
    wait(HB, hs.at[1])
    wait(OA.at[pl.ds(0, 15)], a3s)
    wait(OB.at[pl.ds(0, 7)], b3s)
    wait(FA.at[pl.ds(0, 112)], a4s)
    wait(FB.at[pl.ds(0, 120)], b4s)
    wait(g_core, gs.at[0])
    for k in (1, 2, 3):
        wait(g_z.at[pl.ds(0, 7)], gs.at[k])


def put_out(coarse, gram, coarse_out, gram_out, sems):
    copies = [pltpu.make_async_copy(gram, gram_out, sems.at[4])]
    for k in range(4):
        part = pl.ds(8 * k, 8)
        copies.append(pltpu.make_async_copy(coarse.at[part], coarse_out.at[part], sems.at[k]))
    for copy in copies:
        copy.start()
    for copy in copies:
        copy.wait()


def tiles(*lead):
    return pltpu.VMEM(lead + (ROWS, LANES), BF16)


def shards(fields):
    vmem, dma = pltpu.VMEM, pltpu.SemaphoreType.DMA
    scratch = [
        vmem((32, 64, 256), BF16),
        vmem((4096, 128), F32),
        tiles(128), tiles(128),
        tiles(8, 16), tiles(16, 8),
        tiles(16, 8), tiles(8, 16),
        tiles(2, 4, 8), tiles(2, 4, 8),
        vmem((256, 1024), BF16), vmem((256, 1024), BF16), vmem((128, 1024), BF16), vmem((128, 1024), BF16),
        vmem((768, 256), BF16), vmem((384, 128), BF16), vmem((3, 256, 256), BF16),
        tiles(16, 8), tiles(8, 16),
        tiles(16, 8), tiles(8, 16),
        tiles(128), tiles(128),
        vmem((256, 2048), BF16), vmem((256, 128), F32),
        vmem((32, 128), F32), vmem((16, 128), F32),
        vmem((8, 16, 128), F32), vmem((8, 16, 128), F32), vmem((2, 4, 16, 128), F32),
        dma((4,)), dma((14,)),
        dma(()), dma(()), dma((2,)), dma((2,)),
        dma(()), dma(()), dma((2,)), dma((2,)),
        dma((2,)), dma((2,)),
        dma(()), dma(()), dma((3,)), dma((3,)),
        dma(()), dma(()), dma((8,)), dma((8,)),
        dma((4,)), dma((4,)),
    ]
    coarse, gram = pl.pallas_call(
        kernel,
        name="coarse_grain",
        out_shape=(
            jax.ShapeDtypeStruct((32, 64, 256), BF16),
            jax.ShapeDtypeStruct((64, 64), F32),
        ),
        in_specs=[pl.BlockSpec(memory_space=pltpu.HBM)],
        out_specs=(pl.BlockSpec(memory_space=pltpu.VMEM), pl.BlockSpec(memory_space=pltpu.VMEM)),
        scratch_shapes=scratch,
        compiler_params=pltpu.CompilerParams(
            collective_id=0, has_side_effects=True, vmem_limit_bytes=55_000_000
        ),
    )(fields)
    return pl.pallas_call(
        put_out,
        name="put_out",
        out_shape=(
            jax.ShapeDtypeStruct((32, 64, 256), BF16),
            jax.ShapeDtypeStruct((64, 64), F32),
        ),
        in_specs=[pl.BlockSpec(memory_space=pltpu.VMEM)] * 2,
        out_specs=(pl.BlockSpec(memory_space=pl.ANY), pl.BlockSpec(memory_space=pl.ANY)),
        scratch_shapes=[dma((5,))],
        compiler_params=pltpu.CompilerParams(vmem_limit_bytes=8 << 20),
    )(coarse, gram)


def solution(mesh):
    split = Mesh(mesh.devices.reshape(4, 2, 8, 4, 2), AXES)
    return jax.shard_map(
        shards, mesh=split, in_specs=(P(LON, LAT, None),), out_specs=(P(LON, LAT, None), P()), check_vma=False
    )
```

```python
import numpy as np
import jax
import jax.numpy as jnp
from jax import lax
from jax.experimental import pallas as pl
from jax.experimental.pallas import tpu as pltpu
from jax.sharding import Mesh
from jax.sharding import PartitionSpec as P

AXES = ("X", "H", "Z", "L", "C")
LON = ("X", "H", "Z")
LAT = ("L", "C")
R = 128
NX, NY, NZ = 4, 8, 8
ROWS, LANES = 16, 128
MESH_ID = pl.DeviceIdType.MESH
F32, BF16 = jnp.float32, jnp.bfloat16
NT = (((1,), (1,)), ((), ()))


def taps(distance):
    weight = jnp.exp(-((distance.astype(F32) / R) ** 2))
    return jnp.where(jnp.abs(distance) <= R, weight, 0.0)


def lon_norm():
    d = np.arange(-R, R + 1).astype(np.float32)
    return float(np.sum(np.exp(-((d / R) ** 2)).astype(BF16).astype(np.float32)))


def iota(shape, axis):
    return lax.broadcasted_iota(jnp.int32, shape, axis)


def kernel(
    fields, out, gram,
    FV, T, SA, SB, R1A, R1B, R2A, R2B, HA, HB, XA, XB, XH, SM, AO, AH, W, OA, OB, Q1A, Q1B, FA, FB, MW, GA,
    g_part, g_core, g_z, g_y, g_x,
    ins, loc, a1s, b1s, a1r, b1r, a2s, b2s, a2r, b2r, hs, hr, a3s, b3s, a3r, b3r, a4s, b4s, a4r, b4r, gs, gr,
):
    x, h, z = lax.axis_index("X"), lax.axis_index("H"), lax.axis_index("Z")
    l, c = lax.axis_index("L"), lax.axis_index("C")
    y = h * 4 + l
    yc = y * 2 + c

    def at_z(d):
        return {"Z": (z + d) % NZ}

    def at_yc(dy, dc):
        yy = (y + dy) % NY
        return {"H": yy // 4, "L": yy % 4, "C": (c + dc) % 2}

    def at_xc(dx, dc):
        return {"X": (x + dx) % NX, "C": (c + dc) % 2}

    def send(src, dst, ssem, rsem, device):
        pltpu.make_async_remote_copy(src, dst, ssem, rsem, device_id=device, device_id_type=MESH_ID).start()

    def wait(ref, sem):
        pltpu.make_async_copy(ref, ref, sem).wait()

    def local(src, dst, k):
        copy = pltpu.make_async_copy(src, dst, loc.at[k])
        copy.start()
        return copy

    z_near = [1, 7, 6, 5, 4, 3, 2]
    z_far = [4, 3, 5, 2, 6, 1, 7]
    yc_near = [(dy, dc) for dy in (1, 7, 6, 5, 4, 3, 2, 0) for dc in (0, 1) if (dy, dc) != (0, 0)]
    yc_far = [(dy, dc) for dy in (4, 3, 5, 2, 6, 1, 7, 0) for dc in (0, 1) if (dy, dc) != (0, 0)]
    xc_far = [(2, 0), (2, 1), (1, 0), (3, 0), (1, 1), (3, 1), (0, 1)]

    pieces = []
    for k in range(4):
        pieces.append(pltpu.make_async_copy(fields.at[pl.ds(8 * k, 8)], FV.at[pl.ds(8 * k, 8)], ins.at[k]))
        pieces[k].start()

    barrier = pltpu.get_barrier_semaphore()
    for d in z_far:
        pl.semaphore_signal(barrier, inc=1, device_id=at_z(d), device_id_type=MESH_ID)
    for dy, dc in yc_far:
        pl.semaphore_signal(barrier, inc=1, device_id=at_yc(dy, dc), device_id_type=MESH_ID)
    for dx, dc in xc_far[:6]:
        pl.semaphore_signal(barrier, inc=1, device_id=at_xc(dx, dc), device_id_type=MESH_ID)

    def to_channels(t, carry):
        f = jnp.transpose(FV[pl.ds(t * 2, 2)].reshape(128, 256)).astype(F32)
        u, v, w, b = f[0:64], f[64:128], f[128:192], f[192:256]
        base = pl.multiple_of(t * 256, 256)
        T[pl.ds(base, 64), :] = u * b
        T[pl.ds(base + 64, 64), :] = v * b
        T[pl.ds(base + 128, 64), :] = w * b
        T[pl.ds(base + 192, 64), :] = u * v
        return carry

    for k in range(4):
        pieces[k].wait()
        lax.fori_loop(4 * k, 4 * k + 4, to_channels, 0, unroll=4)

    def pack_of(dst, first_row):
        def pack(k, carry):
            for j in range(8):
                ch = k * 8 + j
                dst[ch] = T[pl.ds(ch + first_row, 16, stride=256), :].astype(BF16)
            return carry

        return pack

    lax.fori_loop(0, 16, pack_of(SB, 128), 0)
    pl.semaphore_wait(barrier, 28)
    for dy, dc in yc_near:
        i = (1 - dy) % 8
        to = ((y + dy) % NY) * 2 + (c + dc) % 2
        send(SB.at[pl.ds(to * 8, 8)], R1B.at[2 * i + c], b1s, b1r.at[i // 4], at_yc(dy, dc))
    own_b1 = local(SB.at[pl.ds(yc * 8, 8)], R1B.at[2 + c], 1)
    lax.fori_loop(0, 16, pack_of(SA, 0), 0)
    for d in z_near:
        i = (1 - d) % 8
        send(SA.at[pl.ds(((z + d) % NZ) * 16, 16)], R1A.at[i], a1s, a1r.at[i // 4], at_z(d))
    own_a1 = local(SA.at[pl.ds(z * 16, 16)], R1A.at[1], 0)

    def lon_matrix(k, carry):
        edge = k // 4
        for block, shift in ((0, 0), (1, -1), (2, 1)):
            row = iota((32, 256), 0) + (k % 4) * 32
            row = row + (1 - edge) * 64 + edge * 128 * (row // 64)
            base = pl.multiple_of(edge * 384 + block * 128 + (k % 4) * 32, 32)
            AO[pl.ds(base, 32), :] = taps(2 * (iota((32, 256), 1) - row) + shift).astype(BF16)
        return carry

    lax.fori_loop(0, 8, lon_matrix, 0)

    def halo_matrix(k, carry):
        for block, shift in ((0, 0), (1, -1), (2, 1)):
            row = iota((32, 128), 0) + k * 32
            row = row + 128 * (row // 64)
            col = iota((32, 128), 1)
            col = jnp.where(col < 64, col - 64, col + 192)
            base = pl.multiple_of(block * 128 + k * 32, 32)
            AH[pl.ds(base, 32), :] = taps(2 * (col - row) + shift).astype(BF16)
        return carry

    lax.fori_loop(0, 4, halo_matrix, 0)

    def lat_matrix(k, carry):
        src = iota((32, 256), 0) + k * 32
        dst = iota((32, 256), 1)
        same = (src // 64) % 2 == (dst // 64) % 2
        apart = 64 * (src // 128 - dst // 128) + src % 64 - dst % 64
        for step in range(3):
            W[step, pl.ds(k * 32, 32), :] = jnp.where(same, taps(apart - 128 * (step - 1)), 0.0).astype(BF16)
        return carry

    lax.fori_loop(0, 8, lat_matrix, 0)
    ones = jnp.ones((16, 256), BF16)
    lat_sums = [jnp.dot(ones, W[k], preferred_element_type=F32)[0:1] for k in range(3)]
    inv_lat = []
    for dst in range(4):
        total = lat_sums[1]
        if dst > 0:
            total = total + lat_sums[2]
        if dst < 3:
            total = total + lat_sums[0]
        inv_lat.append(1.0 / total)
    inv_lon = 1.0 / lon_norm()

    own2 = []
    for g in (0, 1):
        if g == 0:
            own_a1.wait()
            wait(R1A.at[pl.ds(0, 3)], a1r.at[0])
        else:
            wait(R1A.at[pl.ds(0, 4)], a1r.at[1])
        for dy, dc in yc_far:
            to = ((y + dy) % NY) * 2 + (c + dc) % 2
            send(R1A.at[pl.ds(4 * g, 4), to], R2A.at[yc, pl.ds(4 * g, 4)], a2s, a2r.at[g], at_yc(dy, dc))
        own2.append(local(R1A.at[pl.ds(4 * g, 4), yc], R2A.at[yc, pl.ds(4 * g, 4)], 2 + g))
        if g == 0:
            own_b1.wait()
            wait(R1B.at[pl.ds(0, 7)], b1r.at[0])
        else:
            wait(R1B.at[pl.ds(0, 8)], b1r.at[1])
        for d in z_far:
            send(R1B.at[pl.ds(8 * g, 8), (z + d) % NZ], R2B.at[z, pl.ds(8 * g, 8)], b2s, b2r.at[g], at_z(d))
        own2.append(local(R1B.at[pl.ds(8 * g, 8), z], R2B.at[z, pl.ds(8 * g, 8)], 4 + g))

    def halo_a(g):
        own2[2 * g].wait()
        wait(R2A.at[pl.ds(0, 15), pl.ds(0, 4)], a2r.at[g])
        for i in range(4 * g, 4 * g + 4):
            zz = (z + i + 7) % NZ
            hi = zz // 4
            send(R2A.at[pl.ds(hi * 8, 8), i], HA.at[hi, zz % 4], hs.at[0], hr.at[0], at_xc(2 * hi + 3, 0))

    def halo_b(g):
        own2[2 * g + 1].wait()
        wait(R2B.at[pl.ds(0, 7), pl.ds(0, 8)], b2r.at[g])
        for i in range(4 * g, 4 * g + 4):
            yy = (y + i + 7) % NY
            hi = yy // 4
            send(
                R2B.at[pl.ds(hi * 4, 4), pl.ds(2 * i, 2)],
                HB.at[hi, :, pl.ds((yy % 4) * 2, 2)],
                hs.at[1], hr.at[1], at_xc(2 * hi + 3, 0),
            )

    def gather_a(g):
        for i in range(4 * g, 4 * g + 4):
            zz = (z + i + 7) % NZ
            for hh in (0, 1):
                row = pl.multiple_of((8 * hh + zz) * 16, 16)
                for mu in range(8):
                    XA[pl.ds(row, 16), mu * 128 : mu * 128 + 128] = R2A[8 * hh + mu, i]

    def gather_b(g):
        for i in range(4 * g, 4 * g + 4):
            yy = (y + i + 7) % NY
            for zz in range(8):
                row = pl.multiple_of((8 * (yy // 4) + zz) * 16, 16)
                for core in (0, 1):
                    col = pl.multiple_of((2 * (yy % 4) + core) * 128, 128)
                    XB[pl.ds(row, 16), pl.ds(col, 128)] = R2B[zz, 2 * i + core]

    def gather_halo(halo):
        for hi in (0, 1):
            for zz in range(4):
                for mu in range(8):
                    row = (1 - hi) * 64 + zz * 16
                    XH[row : row + 16, mu * 128 : mu * 128 + 128] = halo[hi, zz, mu]

    def filtered(X, edge, store):
        first = iota((128, 128), 1) < 64
        lams = [0, 1, 2, 3, 12, 13, 14, 15] if edge else list(range(4, 12))
        for n in range(4):
            cols = slice(n * 256, n * 256 + 256)
            zs = jnp.dot(AO[edge * 384 : edge * 384 + 384], X[:, cols], preferred_element_type=F32)
            if edge:
                zs = zs + jnp.dot(AH[...], XH[:, cols], preferred_element_type=F32)
            for half in range(2):
                part = zs[:, half * 128 : half * 128 + 128]
                other = jnp.where(first, part[128:256], part[256:384])
                total = part[0:128] + pltpu.roll(other, 64, 1)
                SM[n * 128 : n * 128 + 128, half * 128 : half * 128 + 128] = (total * inv_lon).astype(BF16)
        down = jnp.dot(SM[128:512], W[0], preferred_element_type=F32)
        here = jnp.dot(SM[...], W[1], preferred_element_type=F32)
        up = jnp.dot(SM[0:384], W[2], preferred_element_type=F32)
        for dst in range(4):
            at = dst * 128
            total = here[at : at + 128]
            if dst > 0:
                total = total + up[at - 128 : at]
            if dst < 3:
                total = total + down[at : at + 128]
            total = (total * inv_lat[dst]).astype(BF16)
            for k, lam in enumerate(lams):
                for half in range(2):
                    store(lam, 2 * dst + half, total[k * 16 : k * 16 + 16, half * 128 : half * 128 + 128])

    def store_a(lam, mu, tile):
        OA[(lam // 8) * 8 + mu, lam % 8] = tile

    def store_b(lam, mu, tile):
        OB[lam % 8, (lam // 8) * 8 + mu] = tile

    def part_of(high, part, unit):
        return 4 * unit * (1 - high) if part == 0 else 4 * unit * high + 2 * unit * (part - 1)

    def send_a(part):
        n = 2 if part else 4
        for dy, dc in yc_far:
            yy = (y + dy) % NY
            to = yy * 2 + (c + dc) % 2
            at = pl.ds(part_of(yy // 4, part, 1), n)
            send(OA.at[to, at], Q1A.at[yc, at], a3s, a3r.at[part], at_yc(dy, dc))
        at = pl.ds(part_of(h, part, 1), n)
        return local(OA.at[yc, at], Q1A.at[yc, at], 6 + part)

    def send_b(part):
        n = 4 if part else 8
        for d in z_far:
            zz = (z + d) % NZ
            at = pl.ds(part_of(zz // 4, part, 2), n)
            send(OB.at[zz, at], Q1B.at[z, at], b3s, b3r.at[part], at_z(d))
        at = pl.ds(part_of(z // 4, part, 2), n)
        return local(OB.at[z, at], Q1B.at[z, at], 9 + part)

    halo_a(0)
    halo_b(0)
    gather_a(0)
    gather_b(0)
    halo_a(1)
    gather_a(1)
    filtered(XA, 0, store_a)
    own3 = [send_a(0)]
    halo_b(1)
    gather_b(1)
    filtered(XB, 0, store_b)
    own3.append(send_b(0))
    wait(HA, hr.at[0])
    gather_halo(HA)
    filtered(XA, 1, store_a)
    own3.append(send_a(1))
    own3.append(send_a(2))
    wait(HB, hr.at[1])
    gather_halo(HB)
    filtered(XB, 1, store_b)
    own3.append(send_b(1))
    own3.append(send_b(2))

    for part, ka, kb in ((0, 0, 1), (1, 2, 4), (2, 3, 5)):
        n = 2 if part else 4
        own3[ka].wait()
        wait(Q1A.at[pl.ds(0, 15), pl.ds(0, n)], a3r.at[part])
        for k in range(n):
            zz = part_of(h, part, 1) + (z + k) % n

            @pl.when(zz != z)
            def _():
                there = (zz - z + NZ) % NZ
                send(Q1A.at[:, zz], FA.at[pl.ds(z * 16, 16)], a4s, a4r.at[there], {"Z": zz})

        own3[kb].wait()
        wait(Q1B.at[pl.ds(0, 7), pl.ds(0, 2 * n)], b3r.at[part])
        for k in range(n):
            yy = part_of(z // 4, part, 1) + (y + k) % n
            there = (yy - y + NY) % NY
            for dc in (1, 0):
                cc = (c + dc) % 2

                def send_home():
                    send(
                        Q1B.at[:, yy * 2 + cc], FB.at[pl.ds(yc * 8, 8)], b4s, b4r.at[there],
                        {"H": yy // 4, "L": yy % 4, "C": cc},
                    )

                if dc:
                    send_home()
                else:
                    pl.when(yy != y)(send_home)

    own_a4 = local(Q1A.at[:, z], FA.at[pl.ds(z * 16, 16)], 12)
    own_b4 = local(Q1B.at[:, yc], FB.at[pl.ds(yc * 8, 8)], 13)

    def home(src, ch, row):
        for j in range(16):
            T[pl.ds(row + j, 16, stride=256), :] = src[ch + j].astype(F32)
        row = pl.multiple_of(row, 16)
        for t in range(16):
            MW[pl.ds(row, 16), t * 128 : t * 128 + 128] = T[pl.ds(t * 256 + row, 16), :].astype(BF16)

    own_a4.wait()
    home(FA, z * 16, z * 16)
    own_b4.wait()
    wait(FB.at[pl.ds(0, 8)], b4r.at[0])
    home(FB, y * 16, 128 + y * 16)
    for d in (1, 7, 2, 6, 3, 5, 4):
        wait(FA.at[pl.ds(0, 16)], a4r.at[d])
        zz = (z - d + NZ) % NZ
        home(FA, zz * 16, zz * 16)
        if d == 4:
            GA[0:128] = lax.dot_general(MW[0:128], MW[0:128], NT, preferred_element_type=F32)
        wait(FB.at[pl.ds(0, 16)], b4r.at[d])
        yy = (y - d + NY) % NY
        home(FB, yy * 16, 128 + yy * 16)
    GA[128:256] = lax.dot_general(MW[128:256], MW[128:256], NT, preferred_element_type=F32)

    left = GA[0:64] + GA[128:192]
    right = GA[64:128] + GA[192:256]
    g64 = left + pltpu.roll(right, 64, 1)
    low = iota((32, 128), 1) < 64
    g_part[...] = jnp.where(low, g64[0:32], pltpu.roll(g64[32:64], 64, 1))
    send(g_part.at[pl.ds((1 - c) * 16, 16)], g_core, gs.at[0], gr.at[0], at_yc(0, 1))
    wait(g_core, gr.at[0])
    g_z[z] = g_part[pl.ds(pl.multiple_of(c * 16, 16), 16), :] + g_core[...]
    for d in z_far:
        send(g_z.at[z], g_z.at[z], gs.at[1], gr.at[1], at_z(d))

    def to_cells(t, carry):
        cells = jnp.transpose(MW[:, pl.ds(pl.multiple_of(t * 128, 128), 128)])
        out[pl.ds(t * 2, 2)] = cells.reshape(2, 64, 256)
        return carry

    lax.fori_loop(0, 16, to_cells, 0, unroll=4)

    wait(g_z.at[pl.ds(0, 7)], gr.at[1])
    total = g_z[0]
    for k in range(1, NZ):
        total = total + g_z[k]
    g_y[y] = total
    for d in z_far:
        send(g_y.at[y], g_y.at[y], gs.at[2], gr.at[2], at_yc(d, 0))
    wait(g_y.at[pl.ds(0, 7)], gr.at[2])
    total = g_y[0]
    for k in range(1, NY):
        total = total + g_y[k]
    g_x[c, x] = total * (1.0 / (4 * 2048 * 512))
    for dx, dc in xc_far:
        send(g_x.at[c, x], g_x.at[c, x], gs.at[3], gr.at[3], at_xc(dx, dc))
    wait(g_y.at[pl.ds(0, 7)], gr.at[3])
    for half in range(2):
        total = g_x[half, 0]
        for k in range(1, NX):
            total = total + g_x[half, k]
        gram[half * 16 : half * 16 + 16, :] = total[:, 0:64]
        gram[32 + half * 16 : 48 + half * 16, :] = pltpu.roll(total, 64, 1)[:, 0:64]

    wait(SA.at[pl.ds(0, 112)], a1s)
    wait(SB.at[pl.ds(0, 120)], b1s)
    wait(R2A.at[pl.ds(0, 15)], a2s)
    wait(R2B.at[pl.ds(0, 7)], b2s)
    wait(HA, hs.at[0])
    wait(HB, hs.at[1])
    wait(OA.at[pl.ds(0, 15)], a3s)
    wait(OB.at[pl.ds(0, 7)], b3s)
    wait(FA.at[pl.ds(0, 112)], a4s)
    wait(FB.at[pl.ds(0, 120)], b4s)
    wait(g_core, gs.at[0])
    for k in (1, 2, 3):
        wait(g_z.at[pl.ds(0, 7)], gs.at[k])


def put_out(coarse, gram, coarse_out, gram_out, sems):
    copies = [pltpu.make_async_copy(gram, gram_out, sems.at[4])]
    for k in range(4):
        part = pl.ds(8 * k, 8)
        copies.append(pltpu.make_async_copy(coarse.at[part], coarse_out.at[part], sems.at[k]))
    for copy in copies:
        copy.start()
    for copy in copies:
        copy.wait()


def tiles(*lead):
    return pltpu.VMEM(lead + (ROWS, LANES), BF16)


def shards(fields):
    vmem, dma = pltpu.VMEM, pltpu.SemaphoreType.DMA
    scratch = [
        vmem((32, 64, 256), BF16),
        vmem((4096, 128), F32),
        tiles(128), tiles(128),
        tiles(8, 16), tiles(16, 8),
        tiles(16, 8), tiles(8, 16),
        tiles(2, 4, 8), tiles(2, 4, 8),
        vmem((256, 1024), BF16), vmem((256, 1024), BF16), vmem((128, 1024), BF16), vmem((512, 256), BF16),
        vmem((768, 256), BF16), vmem((384, 128), BF16), vmem((3, 256, 256), BF16),
        tiles(16, 8), tiles(8, 16),
        tiles(16, 8), tiles(8, 16),
        tiles(128), tiles(128),
        vmem((256, 2048), BF16), vmem((256, 128), F32),
        vmem((32, 128), F32), vmem((16, 128), F32),
        vmem((8, 16, 128), F32), vmem((8, 16, 128), F32), vmem((2, 4, 16, 128), F32),
        dma((4,)), dma((14,)),
        dma(()), dma(()), dma((2,)), dma((2,)),
        dma(()), dma(()), dma((2,)), dma((2,)),
        dma((2,)), dma((2,)),
        dma(()), dma(()), dma((3,)), dma((3,)),
        dma(()), dma(()), dma((8,)), dma((8,)),
        dma((4,)), dma((4,)),
    ]
    coarse, gram = pl.pallas_call(
        kernel,
        name="coarse_grain",
        out_shape=(
            jax.ShapeDtypeStruct((32, 64, 256), BF16),
            jax.ShapeDtypeStruct((64, 64), F32),
        ),
        in_specs=[pl.BlockSpec(memory_space=pltpu.HBM)],
        out_specs=(pl.BlockSpec(memory_space=pltpu.VMEM), pl.BlockSpec(memory_space=pltpu.VMEM)),
        scratch_shapes=scratch,
        compiler_params=pltpu.CompilerParams(
            collective_id=0, has_side_effects=True, vmem_limit_bytes=55_000_000
        ),
    )(fields)
    return pl.pallas_call(
        put_out,
        name="put_out",
        out_shape=(
            jax.ShapeDtypeStruct((32, 64, 256), BF16),
            jax.ShapeDtypeStruct((64, 64), F32),
        ),
        in_specs=[pl.BlockSpec(memory_space=pltpu.VMEM)] * 2,
        out_specs=(pl.BlockSpec(memory_space=pl.ANY), pl.BlockSpec(memory_space=pl.ANY)),
        scratch_shapes=[dma((5,))],
        compiler_params=pltpu.CompilerParams(vmem_limit_bytes=8 << 20),
    )(coarse, gram)


def solution(mesh):
    split = Mesh(mesh.devices.reshape(4, 2, 8, 4, 2), AXES)
    return jax.shard_map(
        shards, mesh=split, in_specs=(P(LON, LAT, None),), out_specs=(P(LON, LAT, None), P()), check_vma=False
    )
```
